32 devices in a mesh: dp: 4 (over y, x), atom: 8 (over z, core).
Axes of the slice: x: 2, y: 2, z: 4, core: 2. Of those that a mesh axis runs over, the one named last changes fastest.
Arguments:
- patch_slots: bfloat16 [4, 768, 1024], P('dp', 'atom'), may hold values from -6 to 6
- slot_counts: int32 [4, 8], P('dp'), may hold values from 1 to 96, 256 in all within a row
- dictionary: bfloat16 [1024, 8192], P(None, 'atom')
Outputs:
- sparse_codes: float32 [4, 256, 8192], P('dp', None, 'atom')
- new_dictionary: float32 [1024, 8192], P('dp', 'atom')
The draws below stay inside these ranges and needn't reach their ends.
Inputs may be any that keep to these rules, and one draw needn't show every extreme that they name: `slot_counts`: each row sums to 256 and its largest entry is exactly 96; slots at or beyond a device's count are ignored.
All inputs are finite; a program needn't handle non-finite values.
Results may differ from the reference program's by a relative error of at most 0.0009.
The reference program's roundings to bfloat16 on the way (of `patches`, `code_half` and `residual`) count: a program that leaves them out, or rounds other values in their place, can miss the bound.
Values may be sent and summed in bfloat16 or wider, within the bound.
A program may use at most 64 MiB of HBM per device.

```python
import math
import jax
import jax.numpy as jnp
import numpy as np
from jax import lax

P_SIZE = 1024
B = 256
ITERS = 3
ATOMS = 8192
CAP = 96
N_DP = 4
N_ATOM = 8


def draw_dictionary(key, part):
    first, second = jax.random.split(jax.random.fold_in(key, 11))
    position = jnp.arange(ATOMS, dtype=jnp.float32) / ATOMS
    base = jax.random.normal(first, (P_SIZE, ATOMS), jnp.float32)
    spread = jax.random.uniform(second, (ATOMS,), jnp.float32, math.log(0.8), math.log(1.25))
    column_scale = jnp.exp(position * math.log(3.0) + spread)
    return (base * column_scale[None, :] / math.sqrt(P_SIZE)).astype(jnp.bfloat16)


def shard_levels(rng, dims, cuts, smallest, largest):
    def one(dim, blocks):
        heights = jax.random.uniform(jax.random.fold_in(jax.random.fold_in(rng, 6), dim), (blocks,), jnp.float32, smallest / len(cuts), largest / len(cuts))
        return jnp.repeat(jnp.exp(heights), dims[dim] // blocks).reshape((-1,) + (1,) * (len(dims) - dim - 1))

    gain = one(*cuts[0])
    for cut in cuts[1:]:
        gain = gain * one(*cut)
    return gain


def split_up(number_of, total, most, slope):
    portions = [(1 << 20) // math.isqrt(standing ** slope) + 1 for standing in range(2, number_of + 1)]
    rest, holding = total - most - (number_of - 1), [1] * (number_of - 1)
    while rest > 0:
        movable = [i for i in range(number_of - 1) if holding[i] < most]
        pool, remaining = sum([portions[i] for i in movable]), rest
        for i in movable:
            more = min(most - holding[i], max(1, remaining * portions[i] // pool), rest)
            holding[i] = holding[i] + more
            rest = rest - more
    return np.array([most] + holding)


def uneven(own_key, number_of, total, bound, skew):
    if number_of == 2:
        one = jax.random.randint(own_key, (), max(1, total - bound), min(bound, total - 1) + 1)
        return jnp.stack([one, total - one])
    tallies = jnp.asarray(split_up(number_of, total, bound, skew), jnp.int32)
    couples = (number_of - 1) // 2
    donor, receiver = tallies[1:1 + 2 * couples:2], tallies[2:2 + 2 * couples:2]
    room = jnp.minimum(donor - 1, bound - receiver)
    passed = jax.random.randint(jax.random.fold_in(own_key, 1), (couples,), 0, 1 << 20) % (room + 1)
    tallies = tallies.at[1:1 + 2 * couples:2].set(donor - passed).at[2:2 + 2 * couples:2].set(receiver + passed)
    return tallies[jax.random.permutation(jax.random.fold_in(own_key, 2), number_of)]


def centred(key, shape, scale, reach, pieces=(), kind=jnp.bfloat16):
    level = shard_levels(key, shape, pieces, -0.22, 0.18) if pieces else 1.0
    values = jax.random.normal(key, shape, jnp.float32) * scale * level
    return jnp.minimum(jnp.maximum(values, -reach), reach).astype(kind)


def setup_inputs(seed: int = 0) -> dict:
    splits = jax.random.split(jax.random.key(seed), 4)
    return {
        "patch_slots": centred(splits[0], (N_DP, N_ATOM * CAP, P_SIZE), 1.0, 6.0, ((0, 4), (1, 8))),
        "slot_counts": jax.vmap(lambda own: uneven(own, N_ATOM, B, CAP, 2))(jax.random.split(splits[1], N_DP)).reshape((N_DP, N_ATOM)).astype(jnp.int32),
        "dictionary": draw_dictionary(jax.random.fold_in(splits[3], 71), 0),
    }


def shrink(values):
    return values - jnp.clip(values, -1.0, 1.0)

def compact(slot_rows, counts):
    slot_ends = jnp.cumsum(counts).astype(jnp.int32)
    slot_starts = slot_ends - counts
    position = jnp.arange(B, dtype=jnp.int32)
    owner_index = lax.optimization_barrier(jnp.sum((slot_ends[None, :] <= position[:, None]).astype(jnp.int32), axis=1))
    start_of = slot_starts[owner_index]
    source = (owner_index * CAP + position - start_of).astype(jnp.int32)
    return slot_rows[source]

def reference(patch_slots, slot_counts, dictionary):
    lipschitz = 4.0 * (1.0 + math.sqrt(ATOMS / P_SIZE)) ** 2

    def residual_of(patches, sparse):
        code_half = sparse.astype(jnp.bfloat16)
        recon = jnp.dot(code_half, dictionary.T, preferred_element_type=jnp.float32)
        residual = (recon / lipschitz - patches.astype(jnp.float32)).astype(jnp.bfloat16)
        return (code_half, residual)

    def one_group(gradient, group):
        slot_rows, counts = group
        patches = compact(slot_rows, counts)
        sparse = shrink(jnp.dot(patches, dictionary, preferred_element_type=jnp.float32))
        for step in range(ITERS - 1):
            code_half, residual = residual_of(patches, sparse)
            sparse = shrink(sparse - jnp.dot(residual, dictionary, preferred_element_type=jnp.float32))
        code_half, residual = residual_of(patches, sparse)
        gradient = gradient + jnp.dot(residual.T, code_half, preferred_element_type=jnp.float32)
        return (gradient, sparse)
    start_grad = jnp.zeros((P_SIZE, ATOMS), jnp.float32)
    gradient, sparse_codes = lax.scan(one_group, start_grad, (patch_slots, slot_counts))
    grad_total = jnp.sum(gradient * gradient)
    step_scale = 0.5 * math.sqrt(ATOMS) / jnp.sqrt(grad_total)
    stepped = dictionary.astype(jnp.float32) - step_scale * gradient
    column_sq = lax.optimization_barrier(jnp.sum(stepped * stepped, axis=0))
    new_dictionary = stepped / jnp.sqrt(column_sq + 1e-06)[None, :]
    return (sparse_codes, new_dictionary)
```

```python
import functools
import math

import jax
import jax.numpy as jnp
from jax import lax
from jax.experimental import pallas as pl
from jax.experimental.pallas import tpu as pltpu
from jax.sharding import PartitionSpec as P

B = 256
ITERS = 3
CORES = 2
LINK = jnp.float32
MESH = pl.DeviceIdType.MESH


def shrink(values):
    return values - jnp.clip(values, -1.0, 1.0)


def kernel(
    groups, chips, counts_ref, slots_ref, dict_ref, codes_ref, newd_ref,
    slots_all, gathered, res, half, sib_send, sib_recv, own_part, z_send, z_recv,
    patch, half_recv, rows_res, grad, tot_send, tot_line, tot_dp, col_send, col_recv,
    send_sem, recv_sem,
):
    atoms_dev = chips * CORES
    capacity, share = slots_ref.shape[1], slots_ref.shape[2]
    features = atoms_dev * share
    atom_local = dict_ref.shape[3]
    atoms_total = atom_local * atoms_dev
    lipschitz = 4.0 * (1.0 + math.sqrt(atoms_total / features)) ** 2
    g = lax.axis_index("dp")
    a = lax.axis_index("atom")
    z, k = a // CORES, a % CORES
    other = 1 - k
    sib = a + 1 - 2 * k
    started = []

    def send(src, dst, device):
        i = len(started)
        copy = pltpu.make_async_remote_copy(
            src_ref=src, dst_ref=dst, send_sem=send_sem.at[i], recv_sem=recv_sem.at[i],
            device_id=device, device_id_type=MESH,
        )
        copy.start()
        started.append(copy)
        return copy

    barrier = pltpu.get_barrier_semaphore()
    for r in range(1, atoms_dev):
        pl.semaphore_signal(barrier, inc=1, device_id=(g, (a + r) % atoms_dev), device_id_type=MESH)
    for q in range(1, groups):
        pl.semaphore_signal(barrier, inc=1, device_id=((g + q) % groups, a), device_id_type=MESH)
    pl.semaphore_wait(barrier, atoms_dev - 1 + groups - 1)

    moves = []
    for r in range(1, atoms_dev):
        peer = (a + r) % atoms_dev
        moves.append(send(slots_ref.at[peer], slots_all.at[a], (g, peer)))
    slots_all[a] = slots_ref[a]
    row = lax.broadcasted_iota(jnp.int32, (capacity, B), 0)
    col = lax.broadcasted_iota(jnp.int32, (capacity, B), 1)
    for c in moves:
        c.wait_recv()
    acc = jnp.zeros((share, B), jnp.float32)
    start = jnp.int32(0)
    for j in range(atoms_dev):
        count = counts_ref[j]
        hit = jnp.logical_and(col - start == row, row < count)
        pick = jnp.where(hit, 1.0, 0.0).astype(jnp.bfloat16)
        acc = acc + lax.dot_general(
            slots_all[j], pick, (((0,), (0,)), ((), ())), preferred_element_type=jnp.float32
        )
        start = start + count
    patch[...] = acc
    gathered[0, a] = (-acc).astype(jnp.bfloat16)

    tile = min(256, atom_local)

    def gather_and_code(t):
        direct = []
        for r in range(1, chips):
            direct.append(send(gathered.at[t, a], gathered.at[t, a], (g, (z + r) % chips * CORES + k)))
        pending = [send(gathered.at[t, a], gathered.at[t, a], (g, sib))]
        for r in range(1, chips):
            direct[r - 1].wait_recv()
            src = (z - r + chips) % chips * CORES + k
            pending.append(send(gathered.at[t, src], gathered.at[t, src], (g, sib)))
        for c in pending:
            c.wait_recv()
        res[...] = gathered[t].reshape(features, B).T

        def body(i, _):
            cols = pl.ds(pl.multiple_of(i * tile, tile), tile)
            d = dict_ref[:, :, :, cols].reshape(features, tile)
            prod = jnp.dot(res[...], d, preferred_element_type=jnp.float32)
            if t == 0:
                new = shrink(-prod)
            else:
                new = shrink(codes_ref[:, cols] - prod)
            codes_ref[:, cols] = new
            half[:, cols] = new.astype(jnp.bfloat16)
            return 0

        lax.fori_loop(0, atom_local // tile, body, 0)

    def partial(core):
        d = dict_ref[:, core].reshape(chips * share, atom_local)
        out = lax.dot_general(
            d, half[...], (((1,), (1,)), ((), ())), preferred_element_type=jnp.float32
        )
        return out.reshape(chips, share, B)

    def residual(t):
        sib_send[t] = partial(other)
        order = list(range(chips - 1, -1, -1))
        moves = {}
        for r in order:
            zz = (z + r) % chips
            moves[r] = send(sib_send.at[t, zz], sib_recv.at[t, zz], (g, sib))
        own_part[...] = partial(k)
        arrivals = []
        mine = None
        for r in order:
            zz = (z + r) % chips
            moves[r].wait_recv()
            both = own_part[zz] + sib_recv[t, zz]
            if r == 0:
                mine = both
            else:
                z_send[t, r - 1] = both.astype(LINK)
                arrivals.append(
                    (r, send(z_send.at[t, r - 1], z_recv.at[t, r - 1], (g, zz * CORES + k)))
                )
        for r, c in arrivals:
            c.wait_recv()
            mine = mine + z_recv[t, r - 1].astype(jnp.float32)
        gathered[t + 1, a] = (mine / lipschitz - patch[...]).astype(jnp.bfloat16)

    for t in range(ITERS - 1):
        gather_and_code(t)
        residual(t)
    gather_and_code(ITERS - 1)
    half_moves = []
    for q in range(1, groups):
        half_moves.append(send(half, half_recv.at[q - 1], ((g + q) % groups, a)))
    residual(ITERS - 1)

    direct = []
    for r in range(1, chips):
        direct.append(
            send(gathered.at[ITERS, a], gathered.at[ITERS, a], (g, (z + r) % chips * CORES + k))
        )
    for c in direct:
        c.wait_recv()
    over = []
    for q in range(1, groups):
        d = (g + q) % groups
        over.append(send(gathered.at[ITERS, d * CORES + k], rows_res.at[g, k], (d, a)))
    rows_res[g, k] = gathered[ITERS, g * CORES + k]
    pending = [send(rows_res.at[g, k], rows_res.at[g, k], (g, sib))]
    for q in range(1, groups):
        over[q - 1].wait_recv()
        src = (g - q + groups) % groups
        pending.append(send(rows_res.at[src, k], rows_res.at[src, k], (g, sib)))
    for q in range(groups):
        pending[q].wait_recv()
        src = (g - q + groups) % groups
        if q > 0:
            half_moves[q - 1].wait_recv()
        left = rows_res[src].reshape(CORES * share, B)
        for i in range(atom_local // tile):
            cols = slice(i * tile, (i + 1) * tile)
            right = half[:, cols] if q == 0 else half_recv[q - 1, :, cols]
            prod = jnp.dot(left, right, preferred_element_type=jnp.float32)
            if q == 0:
                grad[:, cols] = prod
            else:
                grad[:, cols] = grad[:, cols] + prod

    value = grad[...]
    total = jnp.sum(jnp.sum(value * value, axis=0, keepdims=True), axis=1, keepdims=True)
    tot_send[0] = jnp.broadcast_to(total, tot_send.shape[1:])
    moves = []
    for r in range(1, atoms_dev):
        moves.append(send(tot_send.at[0], tot_line.at[r - 1], (g, (a + r) % atoms_dev)))
    line = tot_send[0]
    for r in range(1, atoms_dev):
        moves[r - 1].wait_recv()
        line = line + tot_line[r - 1]
    tot_send[1] = line
    moves = []
    for q in range(1, groups):
        moves.append(send(tot_send.at[1], tot_dp.at[q - 1], ((g + q) % groups, a)))
    for q in range(1, groups):
        moves[q - 1].wait_recv()
        line = line + tot_dp[q - 1]
    scale = (0.5 * math.sqrt(atoms_total)) / jnp.sqrt(line[0:1, 0:1])
    own_rows = dict_ref[g].reshape(CORES * share, atom_local).astype(jnp.float32)
    stepped = own_rows - scale * value
    grad[...] = stepped
    column = jnp.sum(stepped * stepped, axis=0, keepdims=True)
    col_send[...] = jnp.broadcast_to(column, col_send.shape)
    moves = []
    for q in range(1, groups):
        moves.append(send(col_send, col_recv.at[q - 1], ((g + q) % groups, a)))
    for q in range(1, groups):
        moves[q - 1].wait_recv()
        column = column + col_recv[q - 1, 0:1, :]
    newd_ref[...] = grad[...] / jnp.sqrt(column + 1e-06)
    for c in started:
        c.wait_send()


def local(groups, chips, patch_slots, slot_counts, dictionary):
    atoms_dev = chips * CORES
    slots = patch_slots[0]
    capacity, features = slots.shape
    share = features // atoms_dev
    atom_local = dictionary.shape[1]
    slots = slots.reshape(capacity, atoms_dev, share).transpose(1, 0, 2)
    blocks = dictionary.reshape(chips, CORES, share, atom_local)
    rows = CORES * share
    copies = (
        (atoms_dev - 1) + ITERS * (2 * chips - 1) + ITERS * (2 * chips - 1)
        + (groups - 1) + (chips - 1) + (2 * groups - 1) + (atoms_dev - 1) + 2 * (groups - 1)
    )
    bf16, f32 = jnp.bfloat16, jnp.float32
    codes, newd = pl.pallas_call(
        functools.partial(kernel, groups, chips),
        out_shape=(
            jax.ShapeDtypeStruct((B, atom_local), f32),
            jax.ShapeDtypeStruct((rows, atom_local), f32),
        ),
        in_specs=[
            pl.BlockSpec(memory_space=pltpu.SMEM),
            pl.BlockSpec(memory_space=pltpu.VMEM),
            pl.BlockSpec(memory_space=pltpu.VMEM),
        ],
        out_specs=(pl.BlockSpec(memory_space=pltpu.VMEM), pl.BlockSpec(memory_space=pltpu.VMEM)),
        scratch_shapes=[
            pltpu.VMEM((atoms_dev, capacity, share), bf16),
            pltpu.VMEM((ITERS + 1, atoms_dev, share, B), bf16),
            pltpu.VMEM((B, features), bf16),
            pltpu.VMEM((B, atom_local), bf16),
            pltpu.VMEM((ITERS, chips, share, B), f32),
            pltpu.VMEM((ITERS, chips, share, B), f32),
            pltpu.VMEM((chips, share, B), f32),
            pltpu.VMEM((ITERS, chips - 1, share, B), LINK),
            pltpu.VMEM((ITERS, chips - 1, share, B), LINK),
            pltpu.VMEM((share, B), f32),
            pltpu.VMEM((groups - 1, B, atom_local), bf16),
            pltpu.VMEM((groups, CORES, share, B), bf16),
            pltpu.VMEM((rows, atom_local), f32),
            pltpu.VMEM((2, 8, 128), f32),
            pltpu.VMEM((atoms_dev - 1, 8, 128), f32),
            pltpu.VMEM((groups - 1, 8, 128), f32),
            pltpu.VMEM((8, atom_local), f32),
            pltpu.VMEM((groups - 1, 8, atom_local), f32),
            pltpu.SemaphoreType.DMA((copies,)),
            pltpu.SemaphoreType.DMA((copies,)),
        ],
        compiler_params=pltpu.CompilerParams(
            collective_id=0, has_side_effects=True, vmem_limit_bytes=48 * 1024 * 1024
        ),
    )(slot_counts[0], slots, blocks)
    return (codes[None], newd)


def solution(mesh):
    groups = mesh.shape["dp"]
    chips = mesh.shape["atom"] // CORES
    assert chips == groups
    placed = (P("dp", "atom", None), P("dp", None), P(None, "atom"))
    return jax.shard_map(
        functools.partial(local, groups, chips),
        mesh=mesh,
        in_specs=placed,
        out_specs=(P("dp", None, "atom"), P("dp", "atom")),
        check_vma=False,
    )
```

```python
import functools
import math

import jax
import jax.numpy as jnp
from jax import lax
from jax.experimental import pallas as pl
from jax.experimental.pallas import tpu as pltpu
from jax.sharding import PartitionSpec as P

B = 256
ITERS = 3
CORES = 2
LINK = jnp.bfloat16
MESH = pl.DeviceIdType.MESH


def shrink(values):
    return values - jnp.clip(values, -1.0, 1.0)


def kernel(
    groups, chips, counts_ref, slots_ref, dict_ref, codes_ref, newd_ref,
    slots_all, gathered, res, half, sib_send, sib_recv, own_part, z_send, z_recv,
    patch, half_recv, rows_res, grad, tot_send, tot_line, tot_dp, col_send, col_recv,
    send_sem, recv_sem,
):
    atoms_dev = chips * CORES
    capacity, share = slots_ref.shape[1], slots_ref.shape[2]
    features = atoms_dev * share
    atom_local = dict_ref.shape[3]
    atoms_total = atom_local * atoms_dev
    lipschitz = 4.0 * (1.0 + math.sqrt(atoms_total / features)) ** 2
    g = lax.axis_index("dp")
    a = lax.axis_index("atom")
    z, k = a // CORES, a % CORES
    other = 1 - k
    sib = a + 1 - 2 * k
    started = []

    def send(src, dst, device):
        i = len(started)
        copy = pltpu.make_async_remote_copy(
            src_ref=src, dst_ref=dst, send_sem=send_sem.at[i], recv_sem=recv_sem.at[i],
            device_id=device, device_id_type=MESH,
        )
        copy.start()
        started.append(copy)
        return copy

    barrier = pltpu.get_barrier_semaphore()
    for r in range(1, atoms_dev):
        pl.semaphore_signal(barrier, inc=1, device_id=(g, (a + r) % atoms_dev), device_id_type=MESH)
    for q in range(1, groups):
        pl.semaphore_signal(barrier, inc=1, device_id=((g + q) % groups, a), device_id_type=MESH)
    pl.semaphore_wait(barrier, atoms_dev - 1 + groups - 1)

    moves = []
    for r in range(1, atoms_dev):
        peer = (a + r) % atoms_dev
        moves.append(send(slots_ref.at[peer], slots_all.at[a], (g, peer)))
    slots_all[a] = slots_ref[a]
    row = lax.broadcasted_iota(jnp.int32, (capacity, B), 0)
    col = lax.broadcasted_iota(jnp.int32, (capacity, B), 1)
    for c in moves:
        c.wait_recv()
    acc = jnp.zeros((share, B), jnp.float32)
    start = jnp.int32(0)
    for j in range(atoms_dev):
        count = counts_ref[j]
        hit = jnp.logical_and(col - start == row, row < count)
        pick = jnp.where(hit, 1.0, 0.0).astype(jnp.bfloat16)
        acc = acc + lax.dot_general(
            slots_all[j], pick, (((0,), (0,)), ((), ())), preferred_element_type=jnp.float32
        )
        start = start + count
    patch[...] = acc
    gathered[0, a] = (-acc).astype(jnp.bfloat16)

    tile = min(256, atom_local)

    def gather_and_code(t):
        direct = []
        for r in range(1, chips):
            direct.append(send(gathered.at[t, a], gathered.at[t, a], (g, (z + r) % chips * CORES + k)))
        pending = [send(gathered.at[t, a], gathered.at[t, a], (g, sib))]
        for r in range(1, chips):
            direct[r - 1].wait_recv()
            src = (z - r + chips) % chips * CORES + k
            pending.append(send(gathered.at[t, src], gathered.at[t, src], (g, sib)))
        for c in pending:
            c.wait_recv()
        res[...] = gathered[t].reshape(features, B).T

        def body(i, _):
            cols = pl.ds(pl.multiple_of(i * tile, tile), tile)
            d = dict_ref[:, :, :, cols].reshape(features, tile)
            prod = jnp.dot(res[...], d, preferred_element_type=jnp.float32)
            if t == 0:
                new = shrink(-prod)
            else:
                new = shrink(codes_ref[:, cols] - prod)
            codes_ref[:, cols] = new
            half[:, cols] = new.astype(jnp.bfloat16)
            return 0

        lax.fori_loop(0, atom_local // tile, body, 0)

    def partial(core):
        d = dict_ref[:, core].reshape(chips * share, atom_local)
        out = lax.dot_general(
            d, half[...], (((1,), (1,)), ((), ())), preferred_element_type=jnp.float32
        )
        return out.reshape(chips, share, B)

    def residual(t):
        sib_send[t] = partial(other)
        order = list(range(chips - 1, -1, -1))
        moves = {}
        for r in order:
            zz = (z + r) % chips
            moves[r] = send(sib_send.at[t, zz], sib_recv.at[t, zz], (g, sib))
        own_part[...] = partial(k)
        arrivals = []
        mine = None
        for r in order:
            zz = (z + r) % chips
            moves[r].wait_recv()
            both = own_part[zz] + sib_recv[t, zz]
            if r == 0:
                mine = both
            else:
                z_send[t, r - 1] = both.astype(LINK)
                arrivals.append(
                    (r, send(z_send.at[t, r - 1], z_recv.at[t, r - 1], (g, zz * CORES + k)))
                )
        for r, c in arrivals:
            c.wait_recv()
            mine = mine + z_recv[t, r - 1].astype(jnp.float32)
        gathered[t + 1, a] = (mine / lipschitz - patch[...]).astype(jnp.bfloat16)

    for t in range(ITERS - 1):
        gather_and_code(t)
        residual(t)
    gather_and_code(ITERS - 1)
    half_moves = []
    for q in range(1, groups):
        half_moves.append(send(half, half_recv.at[q - 1], ((g + q) % groups, a)))
    residual(ITERS - 1)

    direct = []
    for r in range(1, chips):
        direct.append(
            send(gathered.at[ITERS, a], gathered.at[ITERS, a], (g, (z + r) % chips * CORES + k))
        )
    for c in direct:
        c.wait_recv()
    over = []
    for q in range(1, groups):
        d = (g + q) % groups
        over.append(send(gathered.at[ITERS, d * CORES + k], rows_res.at[g, k], (d, a)))
    rows_res[g, k] = gathered[ITERS, g * CORES + k]
    pending = [send(rows_res.at[g, k], rows_res.at[g, k], (g, sib))]
    for q in range(1, groups):
        over[q - 1].wait_recv()
        src = (g - q + groups) % groups
        pending.append(send(rows_res.at[src, k], rows_res.at[src, k], (g, sib)))
    for q in range(groups):
        pending[q].wait_recv()
        src = (g - q + groups) % groups
        if q > 0:
            half_moves[q - 1].wait_recv()
        left = rows_res[src].reshape(CORES * share, B)
        for i in range(atom_local // tile):
            cols = slice(i * tile, (i + 1) * tile)
            right = half[:, cols] if q == 0 else half_recv[q - 1, :, cols]
            prod = jnp.dot(left, right, preferred_element_type=jnp.float32)
            if q == 0:
                grad[:, cols] = prod
            else:
                grad[:, cols] = grad[:, cols] + prod

    value = grad[...]
    total = jnp.sum(jnp.sum(value * value, axis=0, keepdims=True), axis=1, keepdims=True)
    tot_send[0] = jnp.broadcast_to(total, tot_send.shape[1:])
    moves = []
    for r in range(1, atoms_dev):
        moves.append(send(tot_send.at[0], tot_line.at[r - 1], (g, (a + r) % atoms_dev)))
    line = tot_send[0]
    for r in range(1, atoms_dev):
        moves[r - 1].wait_recv()
        line = line + tot_line[r - 1]
    tot_send[1] = line
    moves = []
    for q in range(1, groups):
        moves.append(send(tot_send.at[1], tot_dp.at[q - 1], ((g + q) % groups, a)))
    for q in range(1, groups):
        moves[q - 1].wait_recv()
        line = line + tot_dp[q - 1]
    scale = (0.5 * math.sqrt(atoms_total)) / jnp.sqrt(line[0:1, 0:1])
    own_rows = dict_ref[g].reshape(CORES * share, atom_local).astype(jnp.float32)
    stepped = own_rows - scale * value
    grad[...] = stepped
    column = jnp.sum(stepped * stepped, axis=0, keepdims=True)
    col_send[...] = jnp.broadcast_to(column, col_send.shape)
    moves = []
    for q in range(1, groups):
        moves.append(send(col_send, col_recv.at[q - 1], ((g + q) % groups, a)))
    for q in range(1, groups):
        moves[q - 1].wait_recv()
        column = column + col_recv[q - 1, 0:1, :]
    newd_ref[...] = grad[...] / jnp.sqrt(column + 1e-06)
    for c in started:
        c.wait_send()


def local(groups, chips, patch_slots, slot_counts, dictionary):
    atoms_dev = chips * CORES
    slots = patch_slots[0]
    capacity, features = slots.shape
    share = features // atoms_dev
    atom_local = dictionary.shape[1]
    slots = slots.reshape(capacity, atoms_dev, share).transpose(1, 0, 2)
    blocks = dictionary.reshape(chips, CORES, share, atom_local)
    rows = CORES * share
    copies = (
        (atoms_dev - 1) + ITERS * (2 * chips - 1) + ITERS * (2 * chips - 1)
        + (groups - 1) + (chips - 1) + (2 * groups - 1) + (atoms_dev - 1) + 2 * (groups - 1)
    )
    bf16, f32 = jnp.bfloat16, jnp.float32
    codes, newd = pl.pallas_call(
        functools.partial(kernel, groups, chips),
        out_shape=(
            jax.ShapeDtypeStruct((B, atom_local), f32),
            jax.ShapeDtypeStruct((rows, atom_local), f32),
        ),
        in_specs=[
            pl.BlockSpec(memory_space=pltpu.SMEM),
            pl.BlockSpec(memory_space=pltpu.VMEM),
            pl.BlockSpec(memory_space=pltpu.VMEM),
        ],
        out_specs=(pl.BlockSpec(memory_space=pltpu.VMEM), pl.BlockSpec(memory_space=pltpu.VMEM)),
        scratch_shapes=[
            pltpu.VMEM((atoms_dev, capacity, share), bf16),
            pltpu.VMEM((ITERS + 1, atoms_dev, share, B), bf16),
            pltpu.VMEM((B, features), bf16),
            pltpu.VMEM((B, atom_local), bf16),
            pltpu.VMEM((ITERS, chips, share, B), f32),
            pltpu.VMEM((ITERS, chips, share, B), f32),
            pltpu.VMEM((chips, share, B), f32),
            pltpu.VMEM((ITERS, chips - 1, share, B), LINK),
            pltpu.VMEM((ITERS, chips - 1, share, B), LINK),
            pltpu.VMEM((share, B), f32),
            pltpu.VMEM((groups - 1, B, atom_local), bf16),
            pltpu.VMEM((groups, CORES, share, B), bf16),
            pltpu.VMEM((rows, atom_local), f32),
            pltpu.VMEM((2, 8, 128), f32),
            pltpu.VMEM((atoms_dev - 1, 8, 128), f32),
            pltpu.VMEM((groups - 1, 8, 128), f32),
            pltpu.VMEM((8, atom_local), f32),
            pltpu.VMEM((groups - 1, 8, atom_local), f32),
            pltpu.SemaphoreType.DMA((copies,)),
            pltpu.SemaphoreType.DMA((copies,)),
        ],
        compiler_params=pltpu.CompilerParams(
            collective_id=0, has_side_effects=True, vmem_limit_bytes=48 * 1024 * 1024
        ),
    )(slot_counts[0], slots, blocks)
    return (codes[None], newd)


def solution(mesh):
    groups = mesh.shape["dp"]
    chips = mesh.shape["atom"] // CORES
    assert chips == groups
    placed = (P("dp", "atom", None), P("dp", None), P(None, "atom"))
    return jax.shard_map(
        functools.partial(local, groups, chips),
        mesh=mesh,
        in_specs=placed,
        out_specs=(P("dp", None, "atom"), P("dp", "atom")),
        check_vma=False,
    )
```

```python
import functools
import math

import jax
import jax.numpy as jnp
from jax import lax
from jax.experimental import pallas as pl
from jax.experimental.pallas import tpu as pltpu
from jax.sharding import PartitionSpec as P

B = 256
ITERS = 3
CORES = 2
LINK = jnp.bfloat16
MESH = pl.DeviceIdType.MESH


def shrink(values):
    return values - jnp.clip(values, -1.0, 1.0)


def kernel(
    groups, chips, counts_ref, slots_ref, dict_ref, codes_ref, newd_ref,
    slots_all, gathered, res, half, sib_send, sib_recv, own_part, z_send, z_recv, sent_sum, recv_sum,
    patch, half_recv, rows_res, grad, tot_send, tot_line, tot_dp, col_send, col_recv,
    send_sem, recv_sem,
):
    atoms_dev = chips * CORES
    capacity, share = slots_ref.shape[1], slots_ref.shape[2]
    features = atoms_dev * share
    atom_local = dict_ref.shape[3]
    atoms_total = atom_local * atoms_dev
    lipschitz = 4.0 * (1.0 + math.sqrt(atoms_total / features)) ** 2
    g = lax.axis_index("dp")
    a = lax.axis_index("atom")
    z, k = a // CORES, a % CORES
    other = 1 - k
    sib = a + 1 - 2 * k
    started = []

    def send(src, dst, device):
        i = len(started)
        copy = pltpu.make_async_remote_copy(
            src_ref=src, dst_ref=dst, send_sem=send_sem.at[i], recv_sem=recv_sem.at[i],
            device_id=device, device_id_type=MESH,
        )
        copy.start()
        started.append(copy)
        return copy

    barrier = pltpu.get_barrier_semaphore()
    for r in range(1, atoms_dev):
        pl.semaphore_signal(barrier, inc=1, device_id=(g, (a + r) % atoms_dev), device_id_type=MESH)
    for q in range(1, groups):
        pl.semaphore_signal(barrier, inc=1, device_id=((g + q) % groups, a), device_id_type=MESH)
    pl.semaphore_wait(barrier, atoms_dev - 1 + groups - 1)

    moves = []
    for r in range(1, atoms_dev):
        peer = (a + r) % atoms_dev
        moves.append(send(slots_ref.at[peer], slots_all.at[a], (g, peer)))
    slots_all[a] = slots_ref[a]
    row = lax.broadcasted_iota(jnp.int32, (capacity, B), 0)
    col = lax.broadcasted_iota(jnp.int32, (capacity, B), 1)
    for c in moves:
        c.wait_recv()
    acc = jnp.zeros((share, B), jnp.float32)
    start = jnp.int32(0)
    for j in range(atoms_dev):
        count = counts_ref[j]
        hit = jnp.logical_and(col - start == row, row < count)
        pick = jnp.where(hit, 1.0, 0.0).astype(jnp.bfloat16)
        acc = acc + lax.dot_general(
            slots_all[j], pick, (((0,), (0,)), ((), ())), preferred_element_type=jnp.float32
        )
        start = start + count
    patch[...] = acc
    gathered[0, a] = (-acc).astype(jnp.bfloat16)

    tile = min(256, atom_local)

    def gather_and_code(t):
        direct = []
        for r in range(1, chips):
            direct.append(send(gathered.at[t, a], gathered.at[t, a], (g, (z + r) % chips * CORES + k)))
        pending = [send(gathered.at[t, a], gathered.at[t, a], (g, sib))]
        for r in range(1, chips):
            direct[r - 1].wait_recv()
            src = (z - r + chips) % chips * CORES + k
            pending.append(send(gathered.at[t, src], gathered.at[t, src], (g, sib)))
        for c in pending:
            c.wait_recv()
        res[...] = gathered[t].reshape(features, B).T

        def body(i, _):
            cols = pl.ds(pl.multiple_of(i * tile, tile), tile)
            d = dict_ref[:, :, :, cols].reshape(features, tile)
            prod = jnp.dot(res[...], d, preferred_element_type=jnp.float32)
            if t == 0:
                new = shrink(-prod)
            else:
                new = shrink(codes_ref[:, cols] - prod)
            codes_ref[:, cols] = new
            half[:, cols] = new.astype(jnp.bfloat16)
            return 0

        lax.fori_loop(0, atom_local // tile, body, 0)

    def partial(core):
        d = dict_ref[:, core].reshape(chips * share, atom_local)
        out = lax.dot_general(
            d, half[...], (((1,), (1,)), ((), ())), preferred_element_type=jnp.float32
        )
        return out.reshape(chips, share, B)

    def known(history, t, slot):
        if t == 0:
            return jnp.zeros((share, B), jnp.float32)
        if t == 1:
            return 2.0 * history[0, slot]
        return 2.0 * history[t - 1, slot] - history[t - 2, slot]

    def residual(t):
        sib_send[t] = partial(other)
        order = list(range(chips - 1, -1, -1))
        moves = {}
        for r in order:
            zz = (z + r) % chips
            moves[r] = send(sib_send.at[t, zz], sib_recv.at[t, zz], (g, sib))
        own_part[...] = partial(k)
        arrivals = []
        mine = None
        for r in order:
            zz = (z + r) % chips
            moves[r].wait_recv()
            both = own_part[zz] + sib_recv[t, zz]
            if r == 0:
                mine = both
            else:
                guess = known(sent_sum, t, r - 1)
                step = (both - guess).astype(LINK)
                z_send[t, r - 1] = step
                sent_sum[t, r - 1] = guess + step.astype(jnp.float32)
                arrivals.append(
                    (r, send(z_send.at[t, r - 1], z_recv.at[t, r - 1], (g, zz * CORES + k)))
                )
        for r, c in arrivals:
            c.wait_recv()
            value = known(recv_sum, t, r - 1) + z_recv[t, r - 1].astype(jnp.float32)
            recv_sum[t, r - 1] = value
            mine = mine + value
        gathered[t + 1, a] = (mine / lipschitz - patch[...]).astype(jnp.bfloat16)

    for t in range(ITERS - 1):
        gather_and_code(t)
        residual(t)
    gather_and_code(ITERS - 1)
    half_moves = []
    for q in range(1, groups):
        half_moves.append(send(half, half_recv.at[q - 1], ((g + q) % groups, a)))
    residual(ITERS - 1)

    direct = []
    for r in range(1, chips):
        direct.append(
            send(gathered.at[ITERS, a], gathered.at[ITERS, a], (g, (z + r) % chips * CORES + k))
        )
    for c in direct:
        c.wait_recv()
    over = []
    for q in range(1, groups):
        d = (g + q) % groups
        over.append(send(gathered.at[ITERS, d * CORES + k], rows_res.at[g, k], (d, a)))
    rows_res[g, k] = gathered[ITERS, g * CORES + k]
    pending = [send(rows_res.at[g, k], rows_res.at[g, k], (g, sib))]
    for q in range(1, groups):
        over[q - 1].wait_recv()
        src = (g - q + groups) % groups
        pending.append(send(rows_res.at[src, k], rows_res.at[src, k], (g, sib)))
    for q in range(groups):
        pending[q].wait_recv()
        src = (g - q + groups) % groups
        if q > 0:
            half_moves[q - 1].wait_recv()
        left = rows_res[src].reshape(CORES * share, B)
        for i in range(atom_local // tile):
            cols = slice(i * tile, (i + 1) * tile)
            right = half[:, cols] if q == 0 else half_recv[q - 1, :, cols]
            prod = jnp.dot(left, right, preferred_element_type=jnp.float32)
            if q == 0:
                grad[:, cols] = prod
            else:
                grad[:, cols] = grad[:, cols] + prod

    value = grad[...]
    total = jnp.sum(jnp.sum(value * value, axis=0, keepdims=True), axis=1, keepdims=True)
    tot_send[0] = jnp.broadcast_to(total, tot_send.shape[1:])
    moves = []
    for r in range(1, atoms_dev):
        moves.append(send(tot_send.at[0], tot_line.at[r - 1], (g, (a + r) % atoms_dev)))
    line = tot_send[0]
    for r in range(1, atoms_dev):
        moves[r - 1].wait_recv()
        line = line + tot_line[r - 1]
    tot_send[1] = line
    moves = []
    for q in range(1, groups):
        moves.append(send(tot_send.at[1], tot_dp.at[q - 1], ((g + q) % groups, a)))
    for q in range(1, groups):
        moves[q - 1].wait_recv()
        line = line + tot_dp[q - 1]
    scale = (0.5 * math.sqrt(atoms_total)) / jnp.sqrt(line[0:1, 0:1])
    own_rows = dict_ref[g].reshape(CORES * share, atom_local).astype(jnp.float32)
    stepped = own_rows - scale * value
    grad[...] = stepped
    column = jnp.sum(stepped * stepped, axis=0, keepdims=True)
    col_send[...] = jnp.broadcast_to(column, col_send.shape)
    moves = []
    for q in range(1, groups):
        moves.append(send(col_send, col_recv.at[q - 1], ((g + q) % groups, a)))
    for q in range(1, groups):
        moves[q - 1].wait_recv()
        column = column + col_recv[q - 1, 0:1, :]
    newd_ref[...] = grad[...] / jnp.sqrt(column + 1e-06)
    for c in started:
        c.wait_send()


def local(groups, chips, patch_slots, slot_counts, dictionary):
    atoms_dev = chips * CORES
    slots = patch_slots[0]
    capacity, features = slots.shape
    share = features // atoms_dev
    atom_local = dictionary.shape[1]
    slots = slots.reshape(capacity, atoms_dev, share).transpose(1, 0, 2)
    blocks = dictionary.reshape(chips, CORES, share, atom_local)
    rows = CORES * share
    copies = (
        (atoms_dev - 1) + ITERS * (2 * chips - 1) + ITERS * (2 * chips - 1)
        + (groups - 1) + (chips - 1) + (2 * groups - 1) + (atoms_dev - 1) + 2 * (groups - 1)
    )
    bf16, f32 = jnp.bfloat16, jnp.float32
    codes, newd = pl.pallas_call(
        functools.partial(kernel, groups, chips),
        out_shape=(
            jax.ShapeDtypeStruct((B, atom_local), f32),
            jax.ShapeDtypeStruct((rows, atom_local), f32),
        ),
        in_specs=[
            pl.BlockSpec(memory_space=pltpu.SMEM),
            pl.BlockSpec(memory_space=pltpu.VMEM),
            pl.BlockSpec(memory_space=pltpu.VMEM),
        ],
        out_specs=(pl.BlockSpec(memory_space=pltpu.VMEM), pl.BlockSpec(memory_space=pltpu.VMEM)),
        scratch_shapes=[
            pltpu.VMEM((atoms_dev, capacity, share), bf16),
            pltpu.VMEM((ITERS + 1, atoms_dev, share, B), bf16),
            pltpu.VMEM((B, features), bf16),
            pltpu.VMEM((B, atom_local), bf16),
            pltpu.VMEM((ITERS, chips, share, B), f32),
            pltpu.VMEM((ITERS, chips, share, B), f32),
            pltpu.VMEM((chips, share, B), f32),
            pltpu.VMEM((ITERS, chips - 1, share, B), LINK),
            pltpu.VMEM((ITERS, chips - 1, share, B), LINK),
            pltpu.VMEM((ITERS, chips - 1, share, B), f32),
            pltpu.VMEM((ITERS, chips - 1, share, B), f32),
            pltpu.VMEM((share, B), f32),
            pltpu.VMEM((groups - 1, B, atom_local), bf16),
            pltpu.VMEM((groups, CORES, share, B), bf16),
            pltpu.VMEM((rows, atom_local), f32),
            pltpu.VMEM((2, 8, 128), f32),
            pltpu.VMEM((atoms_dev - 1, 8, 128), f32),
            pltpu.VMEM((groups - 1, 8, 128), f32),
            pltpu.VMEM((8, atom_local), f32),
            pltpu.VMEM((groups - 1, 8, atom_local), f32),
            pltpu.SemaphoreType.DMA((copies,)),
            pltpu.SemaphoreType.DMA((copies,)),
        ],
        compiler_params=pltpu.CompilerParams(
            collective_id=0, has_side_effects=True, vmem_limit_bytes=48 * 1024 * 1024
        ),
    )(slot_counts[0], slots, blocks)
    return (codes[None], newd)


def solution(mesh):
    groups = mesh.shape["dp"]
    chips = mesh.shape["atom"] // CORES
    assert chips == groups
    placed = (P("dp", "atom", None), P("dp", None), P(None, "atom"))
    return jax.shard_map(
        functools.partial(local, groups, chips),
        mesh=mesh,
        in_specs=placed,
        out_specs=(P("dp", None, "atom"), P("dp", "atom")),
        check_vma=False,
    )
```

```python
import functools
import math

import jax
import jax.numpy as jnp
from jax import lax
from jax.experimental import pallas as pl
from jax.experimental.pallas import tpu as pltpu
from jax.sharding import PartitionSpec as P

B = 256
ITERS = 3
CORES = 2
PARTS = 2
LINK = jnp.bfloat16
MESH = pl.DeviceIdType.MESH


def shrink(values):
    return values - jnp.clip(values, -1.0, 1.0)


def kernel(
    groups, chips, counts_ref, slots_ref, dict_ref, codes_ref, newd_ref,
    slots_all, gathered, res, half, sib_send, sib_recv, own_part, z_send, z_recv, sent_sum, recv_sum,
    patch, half_recv, rows_res, grad, tot_send, tot_line, tot_dp, col_send, col_recv,
    send_sem, recv_sem,
):
    atoms_dev = chips * CORES
    capacity, share = slots_ref.shape[1], slots_ref.shape[2]
    features = atoms_dev * share
    atom_local = dict_ref.shape[3]
    atoms_total = atom_local * atoms_dev
    lipschitz = 4.0 * (1.0 + math.sqrt(atoms_total / features)) ** 2
    g = lax.axis_index("dp")
    a = lax.axis_index("atom")
    z, k = a // CORES, a % CORES
    other = 1 - k
    sib = a + 1 - 2 * k
    started = []
    span = B // PARTS

    def send(src, dst, device):
        i = len(started)
        copy = pltpu.make_async_remote_copy(
            src_ref=src, dst_ref=dst, send_sem=send_sem.at[i], recv_sem=recv_sem.at[i],
            device_id=device, device_id_type=MESH,
        )
        copy.start()
        started.append(copy)
        return copy

    barrier = pltpu.get_barrier_semaphore()
    for r in range(1, atoms_dev):
        pl.semaphore_signal(barrier, inc=1, device_id=(g, (a + r) % atoms_dev), device_id_type=MESH)
    for q in range(1, groups):
        pl.semaphore_signal(barrier, inc=1, device_id=((g + q) % groups, a), device_id_type=MESH)
    pl.semaphore_wait(barrier, atoms_dev - 1 + groups - 1)

    moves = []
    for r in range(1, atoms_dev):
        peer = (a + r) % atoms_dev
        moves.append(send(slots_ref.at[peer], slots_all.at[a], (g, peer)))
    slots_all[a] = slots_ref[a]
    row = lax.broadcasted_iota(jnp.int32, (capacity, B), 0)
    col = lax.broadcasted_iota(jnp.int32, (capacity, B), 1)
    for c in moves:
        c.wait_recv()
    acc = jnp.zeros((share, B), jnp.float32)
    start = jnp.int32(0)
    for j in range(atoms_dev):
        count = counts_ref[j]
        hit = jnp.logical_and(col - start == row, row < count)
        pick = jnp.where(hit, 1.0, 0.0).astype(jnp.bfloat16)
        acc = acc + lax.dot_general(
            slots_all[j], pick, (((0,), (0,)), ((), ())), preferred_element_type=jnp.float32
        )
        start = start + count

    tile = min(256, atom_local)
    tiles = atom_local // tile

    def along(t, h):
        return [
            send(gathered.at[t, h, a], gathered.at[t, h, a], (g, (z + r) % chips * CORES + k))
            for r in range(1, chips)
        ]

    def gather_start(t, h):
        direct = along(t, h)
        return direct, [send(gathered.at[t, h, a], gathered.at[t, h, a], (g, sib))]

    def gather_end(t, h, direct, pending):
        for r in range(1, chips):
            direct[r - 1].wait_recv()
            src = (z - r + chips) % chips * CORES + k
            pending.append(send(gathered.at[t, h, src], gathered.at[t, h, src], (g, sib)))
        for c in pending:
            c.wait_recv()

    def code(t, h):
        res[h] = gathered[t, h].reshape(features, span).T
        rows = slice(h * span, (h + 1) * span)

        def body(i, _):
            cols = pl.ds(pl.multiple_of(i * tile, tile), tile)
            d = dict_ref[:, :, :, cols].reshape(features, tile)
            prod = jnp.dot(res[h], d, preferred_element_type=jnp.float32)
            if t == 0:
                new = shrink(-prod)
            else:
                new = shrink(codes_ref[rows, cols] - prod)
            codes_ref[rows, cols] = new
            half[h, :, cols] = new.astype(jnp.bfloat16)
            return 0

        lax.fori_loop(0, tiles, body, 0)

    def partial(h, core):
        d = dict_ref[:, core].reshape(chips * share, atom_local)
        out = lax.dot_general(
            d, half[h], (((1,), (1,)), ((), ())), preferred_element_type=jnp.float32
        )
        return out.reshape(chips, share, span)

    def known(history, t, h, slot):
        if t == 1:
            return 2.0 * history[0, h, slot]
        return 2.0 * history[t - 1, h, slot] - history[t - 2, h, slot]

    order = list(range(chips - 1, -1, -1))

    def recon_start(t, h):
        sib_send[t, h] = partial(h, other)
        moves = {}
        for r in order:
            zz = (z + r) % chips
            moves[r] = send(sib_send.at[t, h, zz], sib_recv.at[t, h, zz], (g, sib))
        own_part[h] = partial(h, k)
        return moves

    def recon_mid(t, h, moves):
        arrivals = []
        mine = None
        for r in order:
            zz = (z + r) % chips
            moves[r].wait_recv()
            both = own_part[h, zz] + sib_recv[t, h, zz]
            if r == 0:
                mine = both
                continue
            dest = zz * CORES + k
            s = r - 1
            if t == 0:
                base = gathered[0, h, dest].astype(jnp.float32)
                fit = jnp.sum(both * base, axis=0, keepdims=True)
                fit = fit / (jnp.sum(base * base, axis=0, keepdims=True) + 1e-30)
                fit = fit.astype(LINK)
                z_send[t, h, s, share:] = jnp.broadcast_to(fit, (16, span))
                guess = fit.astype(jnp.float32) * base
                rows = share + 16
            else:
                guess = known(sent_sum, t, h, s)
                rows = share
            step = (both - guess).astype(LINK)
            z_send[t, h, s, :share] = step
            sent_sum[t, h, s] = guess + step.astype(jnp.float32)
            arrivals.append(
                (s, send(z_send.at[t, h, s, pl.ds(0, rows)], z_recv.at[t, h, s, pl.ds(0, rows)], (g, dest)))
            )
        return mine, arrivals

    def recon_end(t, h, mine, arrivals):
        for s, c in arrivals:
            c.wait_recv()
            if t == 0:
                guess = z_recv[t, h, s, share:share + 1].astype(jnp.float32) * (-patch[h])
            else:
                guess = known(recv_sum, t, h, s)
            value = guess + z_recv[t, h, s, :share].astype(jnp.float32)
            recv_sum[t, h, s] = value
            mine = mine + value
        gathered[t + 1, h, a] = (mine / lipschitz - patch[h]).astype(jnp.bfloat16)

    gathers = []
    for h in range(PARTS):
        patch[h] = acc[:, h * span:(h + 1) * span]
        gathered[0, h, a] = (-patch[h]).astype(jnp.bfloat16)
        gathers.append(gather_start(0, h))
    half_moves = []
    for t in range(ITERS):
        last = t == ITERS - 1
        starts, mids = [], []
        for h in range(PARTS):
            gather_end(t, h, *gathers[h])
            if h > 0:
                mids.append(recon_mid(t, h - 1, starts[h - 1]))
            code(t, h)
            if last:
                for q in range(1, groups):
                    half_moves.append(
                        send(half.at[h], half_recv.at[q - 1, h], ((g + q) % groups, a))
                    )
            starts.append(recon_start(t, h))
        mids.append(recon_mid(t, PARTS - 1, starts[PARTS - 1]))
        gathers = []
        for h in range(PARTS):
            recon_end(t, h, *mids[h])
            gathers.append(along(t + 1, h) if last else gather_start(t + 1, h))

    over, pending = [], []
    for h in range(PARTS):
        for c in gathers[h]:
            c.wait_recv()
        for q in range(1, groups):
            d = (g + q) % groups
            over.append(send(gathered.at[ITERS, h, d * CORES + k], rows_res.at[g, h, k], (d, a)))
        rows_res[g, h, k] = gathered[ITERS, h, g * CORES + k]
        pending.append(send(rows_res.at[g, h, k], rows_res.at[g, h, k], (g, sib)))
    for h in range(PARTS):
        for q in range(1, groups):
            over[h * (groups - 1) + q - 1].wait_recv()
            src = (g - q + groups) % groups
            pending.append(send(rows_res.at[src, h, k], rows_res.at[src, h, k], (g, sib)))
    for c in pending + half_moves:
        c.wait_recv()
    for q in range(groups):
        src = (g - q + groups) % groups
        left = jnp.concatenate(
            [rows_res[src, h].reshape(CORES * share, span) for h in range(PARTS)], axis=1
        )
        for i in range(tiles):
            cols = slice(i * tile, (i + 1) * tile)
            right = half[:, :, cols] if q == 0 else half_recv[q - 1, :, :, cols]
            prod = jnp.dot(left, right.reshape(B, tile), preferred_element_type=jnp.float32)
            if q == 0:
                grad[:, cols] = prod
            else:
                grad[:, cols] = grad[:, cols] + prod

    value = grad[...]
    total = jnp.sum(jnp.sum(value * value, axis=0, keepdims=True), axis=1, keepdims=True)
    tot_send[0] = jnp.broadcast_to(total, tot_send.shape[1:])
    moves = []
    for r in range(1, atoms_dev):
        moves.append(send(tot_send.at[0], tot_line.at[r - 1], (g, (a + r) % atoms_dev)))
    line = tot_send[0]
    for r in range(1, atoms_dev):
        moves[r - 1].wait_recv()
        line = line + tot_line[r - 1]
    tot_send[1] = line
    moves = []
    for q in range(1, groups):
        moves.append(send(tot_send.at[1], tot_dp.at[q - 1], ((g + q) % groups, a)))
    for q in range(1, groups):
        moves[q - 1].wait_recv()
        line = line + tot_dp[q - 1]
    scale = (0.5 * math.sqrt(atoms_total)) / jnp.sqrt(line[0:1, 0:1])
    own_rows = dict_ref[g].reshape(CORES * share, atom_local).astype(jnp.float32)
    stepped = own_rows - scale * value
    grad[...] = stepped
    column = jnp.sum(stepped * stepped, axis=0, keepdims=True)
    col_send[...] = jnp.broadcast_to(column, col_send.shape)
    moves = []
    for q in range(1, groups):
        moves.append(send(col_send, col_recv.at[q - 1], ((g + q) % groups, a)))
    for q in range(1, groups):
        moves[q - 1].wait_recv()
        column = column + col_recv[q - 1, 0:1, :]
    newd_ref[...] = grad[...] / jnp.sqrt(column + 1e-06)
    for c in started:
        c.wait_send()


def local(groups, chips, patch_slots, slot_counts, dictionary):
    atoms_dev = chips * CORES
    slots = patch_slots[0]
    capacity, features = slots.shape
    share = features // atoms_dev
    atom_local = dictionary.shape[1]
    slots = slots.reshape(capacity, atoms_dev, share).transpose(1, 0, 2)
    blocks = dictionary.reshape(chips, CORES, share, atom_local)
    rows = CORES * share
    copies = (
        2 * (atoms_dev - 1) + 2 * (groups - 1)
        + PARTS * (2 * ITERS * (2 * chips - 1) + (chips - 1) + (groups - 1) + (2 * groups - 1))
    )
    span = B // PARTS
    bf16, f32 = jnp.bfloat16, jnp.float32
    codes, newd = pl.pallas_call(
        functools.partial(kernel, groups, chips),
        out_shape=(
            jax.ShapeDtypeStruct((B, atom_local), f32),
            jax.ShapeDtypeStruct((rows, atom_local), f32),
        ),
        in_specs=[
            pl.BlockSpec(memory_space=pltpu.SMEM),
            pl.BlockSpec(memory_space=pltpu.VMEM),
            pl.BlockSpec(memory_space=pltpu.VMEM),
        ],
        out_specs=(pl.BlockSpec(memory_space=pltpu.VMEM), pl.BlockSpec(memory_space=pltpu.VMEM)),
        scratch_shapes=[
            pltpu.VMEM((atoms_dev, capacity, share), bf16),
            pltpu.VMEM((ITERS + 1, PARTS, atoms_dev, share, span), bf16),
            pltpu.VMEM((PARTS, span, features), bf16),
            pltpu.VMEM((PARTS, span, atom_local), bf16),
            pltpu.VMEM((ITERS, PARTS, chips, share, span), f32),
            pltpu.VMEM((ITERS, PARTS, chips, share, span), f32),
            pltpu.VMEM((PARTS, chips, share, span), f32),
            pltpu.VMEM((ITERS, PARTS, chips - 1, share + 16, span), LINK),
            pltpu.VMEM((ITERS, PARTS, chips - 1, share + 16, span), LINK),
            pltpu.VMEM((ITERS, PARTS, chips - 1, share, span), f32),
            pltpu.VMEM((ITERS, PARTS, chips - 1, share, span), f32),
            pltpu.VMEM((PARTS, share, span), f32),
            pltpu.VMEM((groups - 1, PARTS, span, atom_local), bf16),
            pltpu.VMEM((groups, PARTS, CORES, share, span), bf16),
            pltpu.VMEM((rows, atom_local), f32),
            pltpu.VMEM((2, 8, 128), f32),
            pltpu.VMEM((atoms_dev - 1, 8, 128), f32),
            pltpu.VMEM((groups - 1, 8, 128), f32),
            pltpu.VMEM((8, atom_local), f32),
            pltpu.VMEM((groups - 1, 8, atom_local), f32),
            pltpu.SemaphoreType.DMA((copies,)),
            pltpu.SemaphoreType.DMA((copies,)),
        ],
        compiler_params=pltpu.CompilerParams(
            collective_id=0, has_side_effects=True, vmem_limit_bytes=48 * 1024 * 1024
        ),
    )(slot_counts[0], slots, blocks)
    return (codes[None], newd)


def solution(mesh):
    groups = mesh.shape["dp"]
    chips = mesh.shape["atom"] // CORES
    assert chips == groups
    placed = (P("dp", "atom", None), P("dp", None), P(None, "atom"))
    return jax.shard_map(
        functools.partial(local, groups, chips),
        mesh=mesh,
        in_specs=placed,
        out_specs=(P("dp", None, "atom"), P("dp", "atom")),
        check_vma=False,
    )
```

```python
import functools
import math

import jax
import jax.numpy as jnp
from jax import lax
from jax.experimental import pallas as pl
from jax.experimental.pallas import tpu as pltpu
from jax.sharding import PartitionSpec as P

B = 256
ITERS = 3
CORES = 2
PARTS = 2
LINK = jnp.bfloat16
MESH = pl.DeviceIdType.MESH


def shrink(values):
    return values - jnp.clip(values, -1.0, 1.0)


def kernel(
    groups, chips, counts_ref, slots_ref, dict_hbm, codes_hbm, newd_ref, dict_ref, codes_ref,
    slots_all, gathered, res, half, sib_send, sib_recv, own_part, z_send, z_recv, sent_sum, recv_sum,
    patch, half_recv, rows_res, grad, tot_send, tot_line, tot_dp, col_send, col_recv,
    send_sem, recv_sem, load_sem,
):
    atoms_dev = chips * CORES
    capacity, share = slots_all.shape[1], slots_all.shape[2]
    features = atoms_dev * share
    atom_local = dict_ref.shape[3]
    atoms_total = atom_local * atoms_dev
    lipschitz = 4.0 * (1.0 + math.sqrt(atoms_total / features)) ** 2
    g = lax.axis_index("dp")
    a = lax.axis_index("atom")
    z, k = a // CORES, a % CORES
    other = 1 - k
    sib = a + 1 - 2 * k
    started = []
    span = B // PARTS

    def send(src, dst, device):
        i = len(started)
        copy = pltpu.make_async_remote_copy(
            src_ref=src, dst_ref=dst, send_sem=send_sem.at[i], recv_sem=recv_sem.at[i],
            device_id=device, device_id_type=MESH,
        )
        copy.start()
        started.append(copy)
        return copy

    load = pltpu.make_async_copy(dict_hbm, dict_ref, load_sem.at[0])
    load.start()

    def slots_of(device):
        if share % 128:
            return slots_ref.at[device]
        return slots_ref.at[:, pl.ds(pl.multiple_of(device * share, share), share)]

    keep = pltpu.make_async_copy(slots_of(a), slots_all.at[a], load_sem.at[1])
    keep.start()
    barrier = pltpu.get_barrier_semaphore()
    for r in range(1, atoms_dev):
        pl.semaphore_signal(barrier, inc=1, device_id=(g, (a + r) % atoms_dev), device_id_type=MESH)
    for q in range(1, groups):
        pl.semaphore_signal(barrier, inc=1, device_id=((g + q) % groups, a), device_id_type=MESH)
    pl.semaphore_wait(barrier, atoms_dev - 1 + groups - 1)

    moves = []
    for r in range(1, atoms_dev):
        peer = (a + r) % atoms_dev
        moves.append(send(slots_of(peer), slots_all.at[a], (g, peer)))
    row = lax.broadcasted_iota(jnp.int32, (capacity, B), 0)
    col = lax.broadcasted_iota(jnp.int32, (capacity, B), 1)
    for c in moves:
        c.wait_recv()
    keep.wait()
    acc = jnp.zeros((share, B), jnp.float32)
    start = jnp.int32(0)
    for j in range(atoms_dev):
        count = counts_ref[j]
        hit = jnp.logical_and(col - start == row, row < count)
        pick = jnp.where(hit, 1.0, 0.0).astype(jnp.bfloat16)
        acc = acc + lax.dot_general(
            slots_all[j], pick, (((0,), (0,)), ((), ())), preferred_element_type=jnp.float32
        )
        start = start + count

    tile = min(256, atom_local)
    tiles = atom_local // tile

    def along(t, h):
        return [
            send(gathered.at[t, h, a], gathered.at[t, h, a], (g, (z + r) % chips * CORES + k))
            for r in range(1, chips)
        ]

    def gather_start(t, h):
        direct = along(t, h)
        return direct, [send(gathered.at[t, h, a], gathered.at[t, h, a], (g, sib))]

    def gather_end(t, h, direct, pending):
        for r in range(1, chips):
            direct[r - 1].wait_recv()
            src = (z - r + chips) % chips * CORES + k
            pending.append(send(gathered.at[t, h, src], gathered.at[t, h, src], (g, sib)))
        for c in pending:
            c.wait_recv()

    def code(t, h):
        res[h] = gathered[t, h].reshape(features, span).T
        rows = slice(h * span, (h + 1) * span)

        def body(i, _):
            cols = pl.ds(pl.multiple_of(i * tile, tile), tile)
            d = dict_ref[:, :, :, cols].reshape(features, tile)
            prod = jnp.dot(res[h], d, preferred_element_type=jnp.float32)
            if t == 0:
                new = shrink(-prod)
            else:
                new = shrink(codes_ref[rows, cols] - prod)
            codes_ref[rows, cols] = new
            half[h, :, cols] = new.astype(jnp.bfloat16)
            return 0

        lax.fori_loop(0, tiles, body, 0)

    def partial(h, core):
        d = dict_ref[:, core].reshape(chips * share, atom_local)
        out = lax.dot_general(
            d, half[h], (((1,), (1,)), ((), ())), preferred_element_type=jnp.float32
        )
        return out.reshape(chips, share, span)

    def known(history, t, h, slot):
        if t == 1:
            return 2.0 * history[0, h, slot]
        return 2.0 * history[t - 1, h, slot] - history[t - 2, h, slot]

    order = list(range(chips - 1, -1, -1))

    def recon_start(t, h):
        sib_send[t, h] = partial(h, other)
        moves = {}
        for r in order:
            zz = (z + r) % chips
            moves[r] = send(sib_send.at[t, h, zz], sib_recv.at[t, h, zz], (g, sib))
        own_part[h] = partial(h, k)
        return moves

    def recon_mid(t, h, moves):
        arrivals = []
        mine = None
        for r in order:
            zz = (z + r) % chips
            moves[r].wait_recv()
            both = own_part[h, zz] + sib_recv[t, h, zz]
            if r == 0:
                mine = both
                continue
            dest = zz * CORES + k
            s = r - 1
            if t == 0:
                base = gathered[0, h, dest].astype(jnp.float32)
                fit = jnp.sum(both * base, axis=0, keepdims=True)
                fit = fit / (jnp.sum(base * base, axis=0, keepdims=True) + 1e-30)
                fit = fit.astype(LINK)
                z_send[t, h, s, share:] = jnp.broadcast_to(fit, (16, span))
                guess = fit.astype(jnp.float32) * base
                rows = share + 16
            else:
                guess = known(sent_sum, t, h, s)
                rows = share
            step = (both - guess).astype(LINK)
            z_send[t, h, s, :share] = step
            sent_sum[t, h, s] = guess + step.astype(jnp.float32)
            arrivals.append(
                (s, send(z_send.at[t, h, s, pl.ds(0, rows)], z_recv.at[t, h, s, pl.ds(0, rows)], (g, dest)))
            )
        return mine, arrivals

    def recon_end(t, h, mine, arrivals):
        for s, c in arrivals:
            c.wait_recv()
            if t == 0:
                guess = z_recv[t, h, s, share:share + 1].astype(jnp.float32) * (-patch[h])
            else:
                guess = known(recv_sum, t, h, s)
            value = guess + z_recv[t, h, s, :share].astype(jnp.float32)
            recv_sum[t, h, s] = value
            mine = mine + value
        gathered[t + 1, h, a] = (mine / lipschitz - patch[h]).astype(jnp.bfloat16)

    load.wait()
    gathers = []
    for h in range(PARTS):
        patch[h] = acc[:, h * span:(h + 1) * span]
        gathered[0, h, a] = (-patch[h]).astype(jnp.bfloat16)
        gathers.append(gather_start(0, h))
    half_moves = []
    square = groups == 4 and PARTS == 2
    near = [g // 2 * 2 + 1 - g % 2, (g + 2) % 4]
    sources = near + [(near[0] + 2) % 4]

    def relay(h):
        came, onward = (1, 0) if h == 0 else (0, 1)
        half_moves[2 * h + came].wait_recv()
        taken.add(2 * h + came)
        relayed.append(send(half_recv.at[came, h], half_recv.at[2, h], (near[onward], a)))

    taken, relayed, stores = set(), [], []
    for t in range(ITERS):
        last = t == ITERS - 1
        starts, mids = [], []
        for h in range(PARTS):
            gather_end(t, h, *gathers[h])
            if h > 0:
                mids.append(recon_mid(t, h - 1, starts[h - 1]))
            code(t, h)
            if last:
                rows = pl.ds(h * span, span)
                store = pltpu.make_async_copy(
                    codes_ref.at[rows], codes_hbm.at[rows], load_sem.at[2 + h]
                )
                store.start()
                stores.append(store)
            if last and square:
                for q in range(2):
                    half_moves.append(send(half.at[h], half_recv.at[q, h], (near[q], a)))
            elif last:
                for q in range(1, groups):
                    half_moves.append(
                        send(half.at[h], half_recv.at[q - 1, h], ((g + q) % groups, a))
                    )
            starts.append(recon_start(t, h))
        mids.append(recon_mid(t, PARTS - 1, starts[PARTS - 1]))
        if last and square:
            relay(0)
        gathers = []
        for h in range(PARTS):
            recon_end(t, h, *mids[h])
            gathers.append(along(t + 1, h) if last else gather_start(t + 1, h))

    if square:
        relay(1)
    over, pending = [], []
    for h in range(PARTS):
        for c in gathers[h]:
            c.wait_recv()
        for q in range(1, groups):
            d = (g + q) % groups
            over.append(send(gathered.at[ITERS, h, d * CORES + k], rows_res.at[g, h, k], (d, a)))
        rows_res[g, h, k] = gathered[ITERS, h, g * CORES + k]
        pending.append(send(rows_res.at[g, h, k], rows_res.at[g, h, k], (g, sib)))
    for h in range(PARTS):
        for q in range(1, groups):
            over[h * (groups - 1) + q - 1].wait_recv()
            src = (g - q + groups) % groups
            pending.append(send(rows_res.at[src, h, k], rows_res.at[src, h, k], (g, sib)))
    rest = [c for i, c in enumerate(half_moves) if i not in taken]
    for c in pending + rest + relayed:
        c.wait_recv()
    for q in range(groups):
        if square and q:
            src = sources[q - 1]
        else:
            src = (g - q + groups) % groups
        left = jnp.concatenate(
            [rows_res[src, h].reshape(CORES * share, span) for h in range(PARTS)], axis=1
        )
        for i in range(tiles):
            cols = slice(i * tile, (i + 1) * tile)
            right = half[:, :, cols] if q == 0 else half_recv[q - 1, :, :, cols]
            prod = jnp.dot(left, right.reshape(B, tile), preferred_element_type=jnp.float32)
            if q == 0:
                grad[:, cols] = prod
            else:
                grad[:, cols] = grad[:, cols] + prod

    value = grad[...]
    total = jnp.sum(jnp.sum(value * value, axis=0, keepdims=True), axis=1, keepdims=True)
    tot_send[0] = jnp.broadcast_to(total, tot_send.shape[1:])
    moves = []
    for r in range(1, atoms_dev):
        moves.append(send(tot_send.at[0], tot_line.at[r - 1], (g, (a + r) % atoms_dev)))
    line = tot_send[0]
    for r in range(1, atoms_dev):
        moves[r - 1].wait_recv()
        line = line + tot_line[r - 1]
    tot_send[1] = line
    moves = []
    for q in range(1, groups):
        moves.append(send(tot_send.at[1], tot_dp.at[q - 1], ((g + q) % groups, a)))
    for q in range(1, groups):
        moves[q - 1].wait_recv()
        line = line + tot_dp[q - 1]
    scale = (0.5 * math.sqrt(atoms_total)) / jnp.sqrt(line[0:1, 0:1])
    own_rows = dict_ref[g].reshape(CORES * share, atom_local).astype(jnp.float32)
    stepped = own_rows - scale * value
    grad[...] = stepped
    column = jnp.sum(stepped * stepped, axis=0, keepdims=True)
    col_send[...] = jnp.broadcast_to(column, col_send.shape)
    moves = []
    for q in range(1, groups):
        moves.append(send(col_send, col_recv.at[q - 1], ((g + q) % groups, a)))
    for q in range(1, groups):
        moves[q - 1].wait_recv()
        column = column + col_recv[q - 1, 0:1, :]
    newd_ref[...] = grad[...] / jnp.sqrt(column + 1e-06)
    for c in stores:
        c.wait()
    for c in started:
        c.wait_send()


def local(groups, chips, patch_slots, slot_counts, dictionary):
    atoms_dev = chips * CORES
    slots = patch_slots[0]
    capacity, features = slots.shape
    share = features // atoms_dev
    atom_local = dictionary.shape[1]
    if share % 128:
        slots = slots.reshape(capacity, atoms_dev, share).transpose(1, 0, 2)
    blocks = dictionary.reshape(chips, CORES, share, atom_local)
    rows = CORES * share
    copies = (
        2 * (atoms_dev - 1) + 2 * (groups - 1)
        + PARTS * (2 * ITERS * (2 * chips - 1) + (chips - 1) + (groups - 1) + (2 * groups - 1))
    )
    span = B // PARTS
    bf16, f32 = jnp.bfloat16, jnp.float32
    codes, newd = pl.pallas_call(
        functools.partial(kernel, groups, chips),
        out_shape=(
            jax.ShapeDtypeStruct((B, atom_local), f32),
            jax.ShapeDtypeStruct((rows, atom_local), f32),
        ),
        in_specs=[
            pl.BlockSpec(memory_space=pltpu.SMEM),
            pl.BlockSpec(memory_space=pl.ANY),
            pl.BlockSpec(memory_space=pl.ANY),
        ],
        out_specs=(pl.BlockSpec(memory_space=pl.ANY), pl.BlockSpec(memory_space=pltpu.VMEM)),
        scratch_shapes=[
            pltpu.VMEM((chips, CORES, share, atom_local), bf16),
            pltpu.VMEM((B, atom_local), f32),
            pltpu.VMEM((atoms_dev, capacity, share), bf16),
            pltpu.VMEM((ITERS + 1, PARTS, atoms_dev, share, span), bf16),
            pltpu.VMEM((PARTS, span, features), bf16),
            pltpu.VMEM((PARTS, span, atom_local), bf16),
            pltpu.VMEM((ITERS, PARTS, chips, share, span), f32),
            pltpu.VMEM((ITERS, PARTS, chips, share, span), f32),
            pltpu.VMEM((PARTS, chips, share, span), f32),
            pltpu.VMEM((ITERS, PARTS, chips - 1, share + 16, span), LINK),
            pltpu.VMEM((ITERS, PARTS, chips - 1, share + 16, span), LINK),
            pltpu.VMEM((ITERS, PARTS, chips - 1, share, span), f32),
            pltpu.VMEM((ITERS, PARTS, chips - 1, share, span), f32),
            pltpu.VMEM((PARTS, share, span), f32),
            pltpu.VMEM((groups - 1, PARTS, span, atom_local), bf16),
            pltpu.VMEM((groups, PARTS, CORES, share, span), bf16),
            pltpu.VMEM((rows, atom_local), f32),
            pltpu.VMEM((2, 8, 128), f32),
            pltpu.VMEM((atoms_dev - 1, 8, 128), f32),
            pltpu.VMEM((groups - 1, 8, 128), f32),
            pltpu.VMEM((8, atom_local), f32),
            pltpu.VMEM((groups - 1, 8, atom_local), f32),
            pltpu.SemaphoreType.DMA((copies,)),
            pltpu.SemaphoreType.DMA((copies,)),
            pltpu.SemaphoreType.DMA((2 + PARTS,)),
        ],
        compiler_params=pltpu.CompilerParams(
            collective_id=0, has_side_effects=True, vmem_limit_bytes=62 * 1024 * 1024
        ),
    )(slot_counts[0], slots, blocks)
    return (codes[None], newd)


def solution(mesh):
    groups = mesh.shape["dp"]
    chips = mesh.shape["atom"] // CORES
    assert chips == groups
    placed = (P("dp", "atom", None), P("dp", None), P(None, "atom"))
    return jax.shard_map(
        functools.partial(local, groups, chips),
        mesh=mesh,
        in_specs=placed,
        out_specs=(P("dp", None, "atom"), P("dp", "atom")),
        check_vma=False,
    )
```
